128 devices in a mesh: fsdp: 32 (over x, y, core), tensor: 4 (over z).
Axes of the slice: x: 4, y: 4, z: 4, core: 2. Of those that a mesh axis runs over, the one named last changes fastest.
Arguments:
- tokens: bfloat16 [4096, 4096], P(('fsdp', 'tensor')), may hold values from -6 to 6
- gate_blocks: bfloat16 [4, 544, 128, 128], P('tensor', 'fsdp'), may hold values from -0.125 to 0.125
- gate_index: int32 [4, 544], P('tensor', 'fsdp'), may hold values from 0 to 896, as said below
- up_blocks: bfloat16 [4, 544, 128, 128], P('tensor', 'fsdp'), may hold values from -0.125 to 0.125
- up_index: int32 [4, 544], P('tensor', 'fsdp'), may hold values from 0 to 896, as said below
- d_hidden: bfloat16 [4096, 14336], P('fsdp', 'tensor'), may hold values from -6 to 6
Outputs:
- hidden: bfloat16 [4096, 14336], P('fsdp', 'tensor')
- d_tokens: bfloat16 [4096, 4096], P(('fsdp', 'tensor'))
The draws below stay inside these ranges and needn't reach their ends.
Inputs may be any that keep to these rules, and one draw needn't show every extreme that they name: `gate_index`: row t, slots f * 17 to (f + 1) * 17 - 1 belong to fsdp index f: its live slots come first and hold distinct values r * 28 + c with r among row blocks f * 1 to (f + 1) - 1; the remaining slots hold 896. Each such shard has 11 to 17 live slots, both reached in every row; shards 2i and 2i + 1 together hold exactly 28 live slots. `up_index`: as for gate_index, drawn independently.
All inputs are finite; a program needn't handle non-finite values.
Results may differ from the reference program's by a relative error of at most 0.005.
Values may be sent and summed in bfloat16 or wider, within the bound.
No kernel may reach another device: no remote copies, remote signals or barrier semaphores. Data moves between devices by JAX's collectives and lax.ppermute only.
A program may use at most 128 MiB of HBM per device.

```python
import jax
import jax.numpy as jnp
from jax import lax

D = 4096
FF = 14336
BLK = 128
TOKENS = 4096
NRB = 32
NCB = 28
RB = 1
HALF = 14
CAP = 17
SLOTS = 544
N_FSDP = 32
N_TENSOR = 4


def index_draw(key):
    surplus = CAP - HALF
    pair_count = N_FSDP // 2
    key_spread, key_forced, key_side, key_order = jax.random.split(key, 4)
    spread = jax.random.randint(key_spread, (N_TENSOR, pair_count), 0, surplus + 1)
    forced = jax.random.randint(key_forced, (N_TENSOR, 1), 0, pair_count)
    spread = jnp.where(jnp.arange(pair_count)[None, :] == forced, surplus, spread)
    heavy_side = jax.random.randint(key_side, (N_TENSOR, pair_count), 0, 2)
    first_count = HALF + spread * (1 - 2 * heavy_side)
    second_count = 2 * HALF - first_count
    counts = jnp.stack([first_count, second_count], axis=2).reshape(N_TENSOR, N_FSDP)
    shard_keys = jax.random.split(key_order, N_TENSOR * N_FSDP)
    orders = jax.vmap(lambda single: jax.random.permutation(single, RB * NCB))(shard_keys)
    orders = orders[:, :CAP].reshape(N_TENSOR, N_FSDP, CAP)
    offsets = (jnp.arange(N_FSDP) * (RB * NCB))[None, :, None]
    slot_ids = jnp.arange(CAP)[None, None, :]
    block_index = jnp.where(slot_ids < counts[:, :, None], orders + offsets, NRB * NCB)
    return block_index.reshape(N_TENSOR, N_FSDP * CAP).astype(jnp.int32)


def draw_gate_index(key, part):
    return index_draw(jax.random.fold_in(key, 11))


def draw_up_index(key, part):
    return index_draw(jax.random.fold_in(key, 23))


def block_levels(key, shape, cuts, low, high):
    def one(position, blocks):
        draws = jax.random.uniform(jax.random.fold_in(jax.random.fold_in(key, 6), position), (blocks,), jnp.float32, low / len(cuts), high / len(cuts))
        return jnp.repeat(jnp.exp(draws), shape[position] // blocks).reshape((-1,) + (1,) * (len(shape) - position - 1))

    level = one(*cuts[0])
    for cut in cuts[1:]:
        level = level * one(*cut)
    return level


def bell_draw(key, extent, scale, limit, shards=(), kind=jnp.bfloat16):
    values = scale * jax.random.normal(key, extent, jnp.float32)
    if shards:
        values = values * block_levels(key, extent, shards, -0.22, 0.18)
    return jnp.clip(values, -limit, limit).astype(kind)


def setup_inputs(seed: int = 0) -> dict:
    streams_of = jax.random.split(jax.random.key(seed), 7)
    return {
        "tokens": bell_draw(streams_of[0], (TOKENS, D), 1.0, 6.0, ((0, 128),)),
        "gate_blocks": bell_draw(streams_of[1], (N_TENSOR, SLOTS, BLK, BLK), (D // 2) ** -0.5, 0.125, ((0, 4), (1, 32))),
        "gate_index": draw_gate_index(jax.random.fold_in(streams_of[6], 71), 0),
        "up_blocks": bell_draw(streams_of[3], (N_TENSOR, SLOTS, BLK, BLK), (D // 2) ** -0.5, 0.125, ((0, 4), (1, 32))),
        "up_index": draw_up_index(jax.random.fold_in(streams_of[6], 71), 0),
        "d_hidden": bell_draw(streams_of[5], (TOKENS, FF), 1.0, 6.0, ((0, 32), (1, 4))),
    }


def build_panel(blocks_t, index_t):
    dense = jnp.zeros((NRB * NCB, BLK, BLK), blocks_t.dtype).at[index_t].set(blocks_t, mode="drop")
    return dense.reshape(NRB, NCB, BLK, BLK).transpose(0, 2, 1, 3).reshape(D, NCB * BLK)


def reference(tokens, gate_blocks, gate_index, up_blocks, up_index, d_hidden):
    def one_index(dx_total, tensor_id):
        w_gate = build_panel(gate_blocks[tensor_id], gate_index[tensor_id])
        w_up = build_panel(up_blocks[tensor_id], up_index[tensor_id])
        start = (tensor_id * (NCB * BLK)).astype(jnp.int32)
        d_slice = lax.dynamic_slice_in_dim(d_hidden, start, NCB * BLK, 1).astype(jnp.float32)
        gate = jnp.dot(tokens, w_gate, preferred_element_type=jnp.float32)
        up = jnp.dot(tokens, w_up, preferred_element_type=jnp.float32)
        sig = jax.nn.sigmoid(gate)
        active = gate * sig
        hidden_t = (active * up).astype(jnp.bfloat16)
        d_gate = (d_slice * up * sig * (1.0 + gate * (1.0 - sig))).astype(jnp.bfloat16)
        d_up = (d_slice * active).astype(jnp.bfloat16)
        d_part = jnp.dot(d_gate, w_gate.T, preferred_element_type=jnp.float32)
        d_part = d_part + jnp.dot(d_up, w_up.T, preferred_element_type=jnp.float32)
        return dx_total + d_part, hidden_t

    dx_total, hidden_all = lax.scan(one_index, jnp.zeros((TOKENS, D), jnp.float32), jnp.arange(N_TENSOR, dtype=jnp.int32))
    hidden = hidden_all.transpose(1, 0, 2).reshape(TOKENS, FF)
    return hidden, dx_total.astype(jnp.bfloat16)
```

```python
import jax
import jax.numpy as jnp
from jax import lax
from jax.experimental import pallas as pl
from jax.experimental.pallas import tpu as pltpu
from jax.sharding import Mesh, PartitionSpec as P

F32 = jnp.float32
BF16 = jnp.bfloat16
BLK = 128
CHIPS = 16
NCB = 28
CAP = 17
SURE = 11
LIVE = 28
HID = NCB * BLK
WIDTH = CHIPS * 2 * BLK
DEAD = 32 * NCB
SWAP = [(0, 1), (1, 0)]
ANY = pl.BlockSpec(memory_space=pl.ANY)


def params(mib=56):
    return pltpu.CompilerParams(vmem_limit_bytes=mib << 20)


def pack_kernel(scal, mine, theirs, out, sem):
    core, n0 = scal[0], scal[1]

    def copies(first, second):
        made = [
            pltpu.make_async_copy(first.at[pl.ds(0, SURE)], out.at[pl.ds(0, SURE)], sem.at[0]),
            pltpu.make_async_copy(second.at[pl.ds(0, SURE)], out.at[pl.ds(n0, SURE)], sem.at[1]),
        ]
        for j in range(SURE, CAP):
            made.append((j < n0, pltpu.make_async_copy(first.at[j], out.at[j], sem.at[2 + j - SURE])))
            made.append((j < LIVE - n0, pltpu.make_async_copy(second.at[j], out.at[jnp.minimum(n0 + j, LIVE - 1)], sem.at[8 + j - SURE])))
        for verb in ("start", "wait"):
            for m in made:
                if isinstance(m, tuple):
                    pl.when(m[0])(getattr(m[1], verb))
                else:
                    getattr(m, verb)()

    @pl.when(core == 0)
    def _():
        copies(mine, theirs)

    @pl.when(core != 0)
    def _():
        copies(theirs, mine)


def pack(scal, mine, theirs):
    return pl.pallas_call(
        pack_kernel,
        out_shape=jax.ShapeDtypeStruct((LIVE, BLK, BLK), BF16),
        in_specs=[pl.BlockSpec(memory_space=pltpu.SMEM), ANY, ANY],
        out_specs=ANY,
        scratch_shapes=[pltpu.SemaphoreType.DMA((14,))],
        name="pack",
    )(scal, mine, theirs)


def fwd_kernel(table, blocks, x_own, x_other, acc_own, acc_other, panel):
    q = pl.program_id(0)

    @pl.when(q == 0)
    def _():
        acc_own[...] = jnp.zeros_like(acc_own)
        acc_other[...] = jnp.zeros_like(acc_other)

    panel[...] = jnp.zeros_like(panel)
    n0 = jnp.int32(SURE)
    for j in range(SURE, CAP):
        n0 += (table[q, j] < DEAD).astype(jnp.int32)
    base = q * 2 * NCB
    for j in range(LIVE):
        pos = table[q, jnp.where(j < n0, j, CAP + j - n0)] - base
        low = (pos >= NCB).astype(jnp.int32)
        panel[0, pos - low * NCB, pl.ds(pl.multiple_of(low * BLK, BLK), BLK), :] = blocks[j]
    x = jnp.concatenate([x_own[...], x_other[...]], axis=0)
    for c in range(NCB // 2):
        w = jnp.concatenate([panel[0, 2 * c], panel[0, 2 * c + 1]], axis=1)
        r = jnp.dot(x, w, preferred_element_type=F32)
        cols = pl.ds(c * 2 * BLK, 2 * BLK)
        acc_own[:, cols] += r[:BLK]
        acc_other[:, cols] += r[BLK:]


def forward(table, blocks, x_own, x_other):
    return pl.pallas_call(
        fwd_kernel,
        out_shape=(
            jax.ShapeDtypeStruct((BLK, HID), F32),
            jax.ShapeDtypeStruct((BLK, HID), F32),
            jax.ShapeDtypeStruct((CHIPS, NCB, 2 * BLK, BLK), BF16),
        ),
        grid_spec=pltpu.PrefetchScalarGridSpec(
            num_scalar_prefetch=1,
            grid=(CHIPS,),
            in_specs=[
                pl.BlockSpec((LIVE, BLK, BLK), lambda q, t: (q, 0, 0)),
                pl.BlockSpec((BLK, 2 * BLK), lambda q, t: (0, q)),
                pl.BlockSpec((BLK, 2 * BLK), lambda q, t: (0, q)),
            ],
            out_specs=[
                pl.BlockSpec((BLK, HID), lambda q, t: (0, 0)),
                pl.BlockSpec((BLK, HID), lambda q, t: (0, 0)),
                pl.BlockSpec((1, NCB, 2 * BLK, BLK), lambda q, t: (q, 0, 0, 0)),
            ],
        ),
        compiler_params=params(),
        name="forward",
    )(table, blocks, x_own, x_other)


def act_kernel(scal, mine, got, d_hidden, hidden, d_mine, d_send):
    first = scal[0] == 0
    a, b = mine[...], got[...]
    gate = jnp.where(first, a, b)
    up = jnp.where(first, b, a)
    d = d_hidden[...].astype(F32)
    sig = jax.nn.sigmoid(gate)
    active = gate * sig
    hidden[...] = (active * up).astype(BF16)
    d_gate = (d * up * sig * (1.0 + gate * (1.0 - sig))).astype(BF16)
    d_up = (d * active).astype(BF16)
    d_mine[...] = jnp.where(first, d_gate.astype(F32), d_up.astype(F32)).astype(BF16)
    d_send[...] = jnp.where(first, d_up.astype(F32), d_gate.astype(F32)).astype(BF16)


def activate(scal, mine, got, d_hidden):
    steps = 7
    spec = pl.BlockSpec((BLK, HID // steps), lambda i, s: (0, i))
    one = jax.ShapeDtypeStruct((BLK, HID), BF16)
    return pl.pallas_call(
        act_kernel,
        out_shape=(one, one, one),
        grid_spec=pltpu.PrefetchScalarGridSpec(
            num_scalar_prefetch=1, grid=(steps,), in_specs=[spec] * 3, out_specs=[spec] * 3
        ),
        compiler_params=params(),
        name="activate",
    )(scal, mine, got, d_hidden)


def bwd_kernel(d_own, d_other, panel, out_own, out_other, both):
    @pl.when(pl.program_id(0) == 0)
    def _():
        both[:BLK] = d_own[...]
        both[BLK:] = d_other[...]

    w = jnp.concatenate([panel[0, c] for c in range(NCB)], axis=1)
    r = lax.dot_general(both[...], w, (((1,), (1,)), ((), ())), preferred_element_type=F32)
    out_own[...] = r[:BLK]
    out_other[...] = r[BLK:].astype(BF16)


def backward(d_own, d_other, panels):
    whole = pl.BlockSpec((BLK, HID), lambda q: (0, 0))
    return pl.pallas_call(
        bwd_kernel,
        out_shape=(jax.ShapeDtypeStruct((BLK, WIDTH), F32), jax.ShapeDtypeStruct((BLK, WIDTH), BF16)),
        grid=(CHIPS,),
        in_specs=[whole, whole, pl.BlockSpec((1, NCB, 2 * BLK, BLK), lambda q: (q, 0, 0, 0))],
        out_specs=[pl.BlockSpec((BLK, 2 * BLK), lambda q: (0, q))] * 2,
        scratch_shapes=[pltpu.VMEM((2 * BLK, HID), BF16)],
        compiler_params=params(),
        name="backward",
    )(d_own, d_other, panels)


def join_kernel(scal, own, got, keep, *sends):
    z = scal[1]
    rows = BLK // 4
    total = [None] * 4
    for k in range(4):
        at = pl.ds(pl.multiple_of(((z + k) % 4) * rows, rows), rows)
        total[k] = own[at, :] + got[at, :].astype(F32)
    keep[...] = total[0]
    for k in range(3):
        sends[k][...] = total[k + 1].astype(BF16)


def join(scal, own, got):
    rows, steps = BLK // 4, 4
    cols = own.shape[1]
    wide = pl.BlockSpec((BLK, cols // steps), lambda i, s: (0, i))
    thin = pl.BlockSpec((rows, cols // steps), lambda i, s: (0, i))
    return pl.pallas_call(
        join_kernel,
        out_shape=(jax.ShapeDtypeStruct((rows, cols), F32),) + (jax.ShapeDtypeStruct((rows, cols), BF16),) * 3,
        grid_spec=pltpu.PrefetchScalarGridSpec(
            num_scalar_prefetch=1, grid=(steps,), in_specs=[wide, wide], out_specs=[thin] * 4
        ),
        compiler_params=params(),
        name="join",
    )(scal, own, got)


def shards(tokens, gate_blocks, gate_index, up_blocks, up_index, d_hidden):
    core, z = lax.axis_index("c"), lax.axis_index("z")
    first = core == 0
    gate_i, up_i = gate_index[0], up_index[0]
    both_index = lax.all_gather(jnp.stack([gate_i, up_i]), ("x", "y", "c"), axis=0)
    mine = jnp.where(first, gate_blocks[0], up_blocks[0])
    theirs = lax.ppermute(jnp.where(first, up_blocks[0], gate_blocks[0]), "c", SWAP)
    mine_i = jnp.where(first, gate_i, up_i)
    theirs_i = lax.ppermute(jnp.where(first, up_i, gate_i), "c", SWAP)
    n0 = jnp.sum((jnp.where(first, mine_i, theirs_i) < DEAD).astype(jnp.int32))
    payload = pack(jnp.stack([core, n0]), mine, theirs)
    blocks = lax.all_gather(payload, ("x", "y"), axis=0, tiled=True)
    table = jnp.where(first, both_index[:, 0], both_index[:, 1]).reshape(CHIPS, 2 * CAP)
    x_own = lax.all_gather(tokens, "z", axis=0, tiled=True)
    x_other = lax.ppermute(x_own, "c", SWAP)
    acc_own, acc_other, panels = forward(table, blocks, x_own, x_other)
    got = lax.ppermute(acc_other, "c", SWAP)
    scal = jnp.stack([core, z])
    hidden, d_mine, d_send = activate(scal, acc_own, got, d_hidden)
    d_other = lax.ppermute(d_send, "c", SWAP)
    part_own, part_other = backward(d_mine, d_other, panels)
    part_got = lax.ppermute(part_other, "c", SWAP)
    keep, *sends = join(scal, part_own, part_got)
    for k, s in enumerate(sends):
        keep = keep + lax.ppermute(s, "z", [(i, (i + k + 1) % 4) for i in range(4)]).astype(F32)
    return hidden, keep.astype(BF16)


def solution(mesh):
    fine = Mesh(mesh.devices.reshape(4, 4, 2, 4), ("x", "y", "c", "z"))
    fsdp = ("x", "y", "c")
    every = P((*fsdp, "z"), None)
    in_specs = (every, P("z", fsdp, None, None), P("z", fsdp), P("z", fsdp, None, None), P("z", fsdp), P(fsdp, "z"))
    return jax.shard_map(shards, mesh=fine, in_specs=in_specs, out_specs=(P(fsdp, "z"), every), check_vma=False)
```

```python
import jax
import jax.numpy as jnp
from jax import lax
from jax.experimental import pallas as pl
from jax.experimental.pallas import tpu as pltpu
from jax.sharding import Mesh, PartitionSpec as P

F32 = jnp.float32
BF16 = jnp.bfloat16
BLK = 128
CHIPS = 16
NCB = 28
CAP = 17
SURE = 11
LIVE = 28
HID = NCB * BLK
WIDTH = CHIPS * 2 * BLK
DEAD = 32 * NCB
SWAP = [(0, 1), (1, 0)]
HALF = LIVE // 2
UNIT = HALF * BLK + 16
CUT = HALF // 2 * BLK
MARK = HALF * BLK
ROWS = BLK // 4
ANY = pl.BlockSpec(memory_space=pl.ANY)
VMEM = pl.BlockSpec(memory_space=pltpu.VMEM)
SMEM = pl.BlockSpec(memory_space=pltpu.SMEM)


def params(mib=56):
    return pltpu.CompilerParams(vmem_limit_bytes=mib << 20)


def pack_kernel(scal, mine_i, theirs_i, mine, theirs, out_a, out_b):
    core, base = scal[0], scal[1]
    lane = lax.broadcasted_iota(jnp.int32, (16, BLK), 1)

    def place(j, block):
        out, at = (out_a, j) if j < HALF else (out_b, j - HALF)
        out[at * BLK : (at + 1) * BLK] = block

    def fill(first, first_i, second, second_i):
        n0 = jnp.int32(SURE)
        for j in range(SURE, CAP):
            n0 += (first_i[j] < DEAD).astype(jnp.int32)
        marks = [jnp.zeros((16, BLK), jnp.int32)] * 2
        for j in range(LIVE):
            if j < SURE:
                spot = first_i[j]
                place(j, first[j])
            elif j < CAP:
                spot = jnp.where(j < n0, first_i[j], second_i[jnp.maximum(j - n0, 0)])
                pl.when(j < n0)(lambda j=j: place(j, first[j]))
                pl.when(j >= n0)(lambda j=j: place(j, second[jnp.maximum(j - n0, 0)]))
            else:
                spot = second_i[j - n0]
                place(j, second[j - n0])
            half = j // HALF
            marks[half] = jnp.where(lane == j % HALF, spot - base, marks[half])
        out_a[MARK:UNIT] = marks[0].astype(F32).astype(BF16)
        out_b[MARK:UNIT] = marks[1].astype(F32).astype(BF16)

    pl.when(core == 0)(lambda: fill(mine, mine_i, theirs, theirs_i))
    pl.when(core != 0)(lambda: fill(theirs, theirs_i, mine, mine_i))


def pack(scal, mine_i, theirs_i, mine, theirs):
    one = jax.ShapeDtypeStruct((UNIT, BLK), BF16)
    return pl.pallas_call(
        pack_kernel,
        out_shape=(one, one),
        in_specs=[SMEM, SMEM, SMEM, VMEM, VMEM],
        out_specs=(VMEM, VMEM),
        compiler_params=params(),
        name="pack",
    )(scal, mine_i, theirs_i, mine, theirs)


def forward(units, chips, x_own, x_other, pieces, carry=None, room=None):
    count, given = len(units), len(pieces)
    room = room or count
    resumed = carry is not None

    def kernel(chip_of, xo, xt, *refs):
        parts, refs = refs[:given], refs[given:]
        if resumed:
            before, refs = refs[:2], refs[2:]
        acc_own, acc_other, panels, buf, tiles, ints, marks, panel, sem_t, sem_b, sem_m, sem_p, sem_a = refs
        moved = []
        for t, pair in enumerate(units):
            for h, source in enumerate(pair):
                part, row, rows, at = source[-1]
                mark = row + MARK - at
                tile = pltpu.make_async_copy(parts[part].at[pl.ds(mark, 16)], tiles.at[2 * t + h], sem_t.at[2 * t + h])
                tile.start()
                moved.append(tile)
        for t, pair in enumerate(units):
            for h, source in enumerate(pair):
                for part, row, rows, at in source:
                    pltpu.make_async_copy(
                        parts[part].at[pl.ds(row, rows)], buf.at[t, h, pl.ds(at, rows)], sem_b.at[t, h]
                    ).start()
        if resumed:
            loads = [pltpu.make_async_copy(b, a, sem_a.at[i]) for i, (b, a) in enumerate(zip(before, (acc_own, acc_other)))]
            for m in loads:
                m.start()
        else:
            acc_own[...] = jnp.zeros_like(acc_own)
            acc_other[...] = jnp.zeros_like(acc_other)
        for i, m in enumerate(moved):
            m.wait()
            ints[pl.ds(i, 1), :] = tiles[i].astype(F32)[0:1].astype(jnp.int32)
        load = pltpu.make_async_copy(ints, marks, sem_m)
        load.start()
        load.wait()
        if resumed:
            for m in loads:
                m.wait()

        def stored(slot):
            return pltpu.make_async_copy(panel.at[slot], panels.at[0], sem_p.at[slot])

        def step(t, _):
            slot = t % 2
            for h in range(2):
                pltpu.make_async_copy(buf.at[t, h], buf.at[t, h], sem_b.at[t, h]).wait()
            pl.when(t >= 2)(lambda: stored(slot).wait())
            panel[slot] = jnp.zeros((NCB, 2 * BLK, BLK), BF16)
            for j in range(LIVE):
                h, k = divmod(j, HALF)
                pos = marks[2 * t + h, k]
                low = (pos >= NCB).astype(jnp.int32)
                panel[slot, pos - low * NCB, pl.ds(pl.multiple_of(low * BLK, BLK), BLK), :] = buf[t, h, k * BLK : (k + 1) * BLK]
            pltpu.make_async_copy(panel.at[slot], panels.at[room - count + t], sem_p.at[slot]).start()
            cols = pl.ds(pl.multiple_of(chip_of[t] * 2 * BLK, 2 * BLK), 2 * BLK)
            x = jnp.concatenate([xo[:, cols], xt[:, cols]], axis=0)
            for c in range(NCB // 2):
                w = jnp.concatenate([panel[slot, 2 * c], panel[slot, 2 * c + 1]], axis=1)
                r = jnp.dot(x, w, preferred_element_type=F32)
                at = pl.ds(c * 2 * BLK, 2 * BLK)
                acc_own[:, at] += r[:BLK]
                acc_other[:, at] += r[BLK:]
            return 0

        lax.fori_loop(0, count, step, 0)
        for t in range(max(0, count - 2), count):
            stored(t % 2).wait()

    extra = list(carry) if resumed else []
    alias = {3 + given + 2: 2} if resumed and len(extra) == 3 else {}
    acc = jax.ShapeDtypeStruct((BLK, HID), F32)
    wrapped = kernel
    if alias:
        def wrapped(*refs):
            kernel(*refs[: 3 + given + 2], *refs[3 + given + 3 :])
    return pl.pallas_call(
        wrapped,
        out_shape=(acc, acc, jax.ShapeDtypeStruct((room, NCB, 2 * BLK, BLK), BF16)),
        in_specs=[SMEM, VMEM, VMEM] + [ANY] * (given + len(extra)),
        out_specs=(VMEM, VMEM, ANY),
        scratch_shapes=[
            pltpu.VMEM((count, 2, UNIT, BLK), BF16),
            pltpu.VMEM((2 * count, 16, BLK), BF16),
            pltpu.VMEM((2 * count, BLK), jnp.int32),
            pltpu.SMEM((2 * count, BLK), jnp.int32),
            pltpu.VMEM((2, NCB, 2 * BLK, BLK), BF16),
            pltpu.SemaphoreType.DMA((2 * count,)),
            pltpu.SemaphoreType.DMA((count, 2)),
            pltpu.SemaphoreType.DMA,
            pltpu.SemaphoreType.DMA((2,)),
            pltpu.SemaphoreType.DMA((2,)),
        ],
        input_output_aliases=alias,
        compiler_params=params(),
        name="forward",
    )(chips, x_own, x_other, *pieces, *extra)


def act_kernel(scal, mine, got, d_hidden, hidden, d_mine, d_send):
    def work(gate_ref, up_ref, d_gate, d_up):
        for k in range(4):
            rel = pl.ds(k * ROWS, ROWS)
            real = pl.ds(pl.multiple_of((scal[1] - k + 4) % 4 * ROWS, ROWS), ROWS)
            gate, up = gate_ref[rel, :], up_ref[rel, :]
            d = d_hidden[real, :].astype(F32)
            sig = jax.nn.sigmoid(gate)
            active = gate * sig
            hidden[real, :] = (active * up).astype(BF16)
            d_gate[rel, :] = (d * up * sig * (1.0 + gate * (1.0 - sig))).astype(BF16)
            d_up[rel, :] = (d * active).astype(BF16)

    pl.when(scal[0] == 0)(lambda: work(mine, got, d_mine, d_send))
    pl.when(scal[0] != 0)(lambda: work(got, mine, d_send, d_mine))


def activate(scal, mine, got, d_hidden):
    steps = 7
    spec = pl.BlockSpec((BLK, HID // steps), lambda i, s: (0, i))
    one = jax.ShapeDtypeStruct((BLK, HID), BF16)
    return pl.pallas_call(
        act_kernel,
        out_shape=(one, one, one),
        grid_spec=pltpu.PrefetchScalarGridSpec(
            num_scalar_prefetch=1, grid=(steps,), in_specs=[spec] * 3, out_specs=[spec] * 3
        ),
        compiler_params=params(),
        name="activate",
    )(scal, mine, got, d_hidden)


def bwd_kernel(d_own, d_other, panel, out_own, out_other, both):
    @pl.when(pl.program_id(0) == 0)
    def _():
        both[:BLK] = d_own[...]
        both[BLK:] = d_other[...]

    w = jnp.concatenate([panel[0, c] for c in range(NCB)], axis=1)
    r = lax.dot_general(both[...], w, (((1,), (1,)), ((), ())), preferred_element_type=F32)
    out_own[...] = r[:BLK]
    out_other[...] = r[BLK:].astype(BF16)


def backward(d_own, d_other, panels):
    whole = pl.BlockSpec((BLK, HID), lambda q: (0, 0))
    count = panels.shape[0]
    width = count * 2 * BLK
    return pl.pallas_call(
        bwd_kernel,
        out_shape=(jax.ShapeDtypeStruct((BLK, width), F32), jax.ShapeDtypeStruct((BLK, width), BF16)),
        grid=(count,),
        in_specs=[whole, whole, pl.BlockSpec((1, NCB, 2 * BLK, BLK), lambda q: (q, 0, 0, 0))],
        out_specs=[pl.BlockSpec((BLK, 2 * BLK), lambda q: (0, q))] * 2,
        scratch_shapes=[pltpu.VMEM((2 * BLK, HID), BF16)],
        compiler_params=params(),
        name="backward",
    )(d_own, d_other, panels)


def join_kernel(own, got, keep, *sends):
    for k in range(4):
        at = slice(k * ROWS, (k + 1) * ROWS)
        total = own[at, :] + got[at, :].astype(F32)
        if k:
            sends[k - 1][...] = total.astype(BF16)
        else:
            keep[...] = total


def join(own, got):
    cols = own.shape[1]
    return pl.pallas_call(
        join_kernel,
        out_shape=(jax.ShapeDtypeStruct((ROWS, cols), F32),) + (jax.ShapeDtypeStruct((ROWS, cols), BF16),) * 3,
        in_specs=[VMEM, VMEM],
        out_specs=(VMEM,) * 4,
        compiler_params=params(),
        name="join",
    )(own, got)


def finish(chips, groups):
    def kernel(chip_of, *refs):
        out, t = refs[-1], 0
        for g in range(len(groups)):
            parts = refs[4 * g : 4 * g + 4]
            for i in range(parts[0].shape[1] // (2 * BLK)):
                at = slice(i * 2 * BLK, (i + 1) * 2 * BLK)
                total = parts[0][:, at]
                for p in parts[1:]:
                    total += p[:, at].astype(F32)
                out[:, pl.ds(pl.multiple_of(chip_of[t] * 2 * BLK, 2 * BLK), 2 * BLK)] = total.astype(BF16)
                t += 1

    flat = [a for g in groups for a in g]
    return pl.pallas_call(
        kernel,
        out_shape=jax.ShapeDtypeStruct((ROWS, WIDTH), BF16),
        in_specs=[SMEM] + [VMEM] * len(flat),
        out_specs=VMEM,
        compiler_params=params(),
        name="finish",
    )(chips, *flat)


def shift(a, axis, by):
    return lax.ppermute(a, axis, [(i, (i + by) % 4) for i in range(4)])


def shards(tokens, gate_blocks, gate_index, up_blocks, up_index, d_hidden):
    x, y, core, z = (lax.axis_index(n) for n in ("x", "y", "c", "z"))
    first = core == 0
    gate_i, up_i = gate_index[0], up_index[0]
    theirs = lax.ppermute(jnp.where(first, up_blocks[0], gate_blocks[0]), "c", SWAP)
    theirs_i = lax.ppermute(jnp.where(first, up_i, gate_i), "c", SWAP)
    mine = jnp.where(first, gate_blocks[0], up_blocks[0])
    mine_i = jnp.where(first, gate_i, up_i)
    scal = jnp.stack([core, z, (x * 4 + y) * 2 * NCB])
    a, b = pack(scal[0::2], mine_i, theirs_i, mine, theirs)

    line = {}
    for name, unit, near in (("a", a, "x"), ("b", b, "y")):
        line[name] = [unit, shift(unit, near, 1), shift(unit, near, -1), shift(unit, near, 2)]
    x_own = jnp.concatenate([tokens] + [shift(tokens, "z", k) for k in (1, 2, 3)], axis=0)
    x_other = lax.ppermute(x_own, "c", SWAP)
    three, far = {}, {}
    for name, across in (("a", "y"), ("b", "x")):
        u = line[name]
        own3 = jnp.concatenate(u[:3], axis=0)
        three[name] = [None, shift(own3, across, 1), shift(own3, across, -1)]
        far[name] = [u[3], shift(u[3], across, 1), shift(u[3], across, -1)]
    middle = UNIT + CUT
    three2, far2 = {}, {}
    for name, across in (("a", "y"), ("b", "x")):
        t, f = three[name], far[name]
        three2[name] = (shift(t[1][:middle], across, 1), shift(t[2][middle:], across, -1))
        far2[name] = (shift(f[1][:CUT], across, 1), shift(f[2][CUT:], across, -1))

    def source(name, near, across):
        if across == 0:
            return [(line[name][near], 0, UNIT, 0)]
        if across < 3 and near < 3:
            return [(three[name][across], near * UNIT, UNIT, 0)]
        if across < 3:
            return [(far[name][across], 0, UNIT, 0)]
        if near == 3:
            low, high = far2[name]
            return [(low, 0, CUT, 0), (high, 0, UNIT - CUT, CUT)]
        low, high = three2[name]
        if near == 0:
            return [(low, 0, UNIT, 0)]
        if near == 2:
            return [(high, UNIT - CUT, UNIT, 0)]
        return [(low, UNIT, CUT, 0), (high, 0, UNIT - CUT, CUT)]

    step = (0, -1, 1, 2)
    near9 = [(i, j) for i in range(3) for j in range(3)]
    last6 = [(3, 0), (3, 1), (3, 2), (0, 3), (1, 3), (2, 3)]
    order = near9 + last6 + [(3, 3)]
    chips = jnp.stack([(x + step[i]) % 4 * 4 + (y + step[j]) % 4 for i, j in order])

    def stage(which, at, carry=None, room=None):
        pieces, units = [], []
        for i, j in which:
            pair = []
            for src in (source("a", i, j), source("b", j, i)):
                row = []
                for piece, r, n, d in src:
                    k = next((m for m, p in enumerate(pieces) if p is piece), None)
                    if k is None:
                        k = len(pieces)
                        pieces.append(piece)
                    row.append((k, r, n, d))
                pair.append(row)
            units.append(pair)
        return forward(units, chips[at : at + len(which)], x_own, x_other, pieces, carry, room)

    acc_own, acc_other, panels9 = stage(near9, 0)
    acc_own, acc_other, panels7 = stage(last6, 9, (acc_own, acc_other), None)
    acc_own, acc_other, panels1 = stage([(3, 3)], 15, (acc_own, acc_other), None)
    got = lax.ppermute(acc_other, "c", SWAP)
    hidden, d_mine, d_send = activate(scal[:2], acc_own, got, d_hidden)
    d_other = lax.ppermute(d_send, "c", SWAP)
    groups = []
    for panels in (panels9, panels7, panels1):
        part_own, part_other = backward(d_mine, d_other, panels)
        keep, *sends = join(part_own, lax.ppermute(part_other, "c", SWAP))
        groups.append([keep] + [shift(s, "z", -k - 1) for k, s in enumerate(sends)])
    return hidden, finish(chips, groups)

def solution(mesh):
    fine = Mesh(mesh.devices.reshape(4, 4, 2, 4), ("x", "y", "c", "z"))
    fsdp = ("x", "y", "c")
    every = P((*fsdp, "z"), None)
    in_specs = (every, P("z", fsdp, None, None), P("z", fsdp), P("z", fsdp, None, None), P("z", fsdp), P(fsdp, "z"))
    return jax.shard_map(shards, mesh=fine, in_specs=in_specs, out_specs=(P(fsdp, "z"), every), check_vma=False)
```

```python
import jax
import jax.numpy as jnp
from jax import lax
from jax.experimental import pallas as pl
from jax.experimental.pallas import tpu as pltpu
from jax.sharding import Mesh, PartitionSpec as P

F32 = jnp.float32
BF16 = jnp.bfloat16
BLK = 128
CHIPS = 16
NCB = 28
CAP = 17
SURE = 11
LIVE = 28
HID = NCB * BLK
WIDTH = CHIPS * 2 * BLK
DEAD = 32 * NCB
SWAP = [(0, 1), (1, 0)]
HALF = LIVE // 2
UNIT = HALF * BLK + 16
MARK = HALF * BLK
ROWS = BLK // 4
HBM = pl.BlockSpec(memory_space=pltpu.HBM)
VMEM = pl.BlockSpec(memory_space=pltpu.VMEM)
SMEM = pl.BlockSpec(memory_space=pltpu.SMEM)


def params(mib=56):
    return pltpu.CompilerParams(vmem_limit_bytes=mib << 20)


def pack_kernel(scal, mine_i, theirs_i, mine, theirs, out_a, out_b):
    core, base = scal[0], scal[1]
    lane = lax.broadcasted_iota(jnp.int32, (16, BLK), 1)

    def place(j, block):
        out, at = (out_a, j) if j < HALF else (out_b, j - HALF)
        out[at * BLK : (at + 1) * BLK] = block

    def fill(first, first_i, second, second_i):
        n0 = jnp.int32(SURE)
        for j in range(SURE, CAP):
            n0 += (first_i[j] < DEAD).astype(jnp.int32)
        marks = [jnp.zeros((16, BLK), jnp.int32)] * 2
        for j in range(LIVE):
            if j < SURE:
                spot = first_i[j]
                place(j, first[j])
            elif j < CAP:
                spot = jnp.where(j < n0, first_i[j], second_i[jnp.maximum(j - n0, 0)])
                pl.when(j < n0)(lambda j=j: place(j, first[j]))
                pl.when(j >= n0)(lambda j=j: place(j, second[jnp.maximum(j - n0, 0)]))
            else:
                spot = second_i[j - n0]
                place(j, second[j - n0])
            half = j // HALF
            marks[half] = jnp.where(lane == j % HALF, spot - base, marks[half])
        out_a[MARK:UNIT] = marks[0].astype(F32).astype(BF16)
        out_b[MARK:UNIT] = marks[1].astype(F32).astype(BF16)

    pl.when(core == 0)(lambda: fill(mine, mine_i, theirs, theirs_i))
    pl.when(core != 0)(lambda: fill(theirs, theirs_i, mine, mine_i))


def pack(scal, mine_i, theirs_i, mine, theirs):
    one = jax.ShapeDtypeStruct((UNIT, BLK), BF16)
    return pl.pallas_call(
        pack_kernel,
        out_shape=(one, one),
        in_specs=[SMEM, SMEM, SMEM, VMEM, VMEM],
        out_specs=(VMEM, VMEM),
        compiler_params=params(8),
        cost_estimate=cost(2),
        name="pack",
    )(scal, mine_i, theirs_i, mine, theirs)


def stack_kernel(a, b, c, d, first, second):
    first[:UNIT] = a[...]
    first[UNIT:] = b[...]
    second[:UNIT] = c[...]
    second[UNIT:] = d[...]


def stack_pairs(a, b, c, d):
    two = pltpu.VMEM((2 * UNIT, BLK), BF16)
    return pl.pallas_call(
        stack_kernel,
        out_shape=(two, two),
        in_specs=[VMEM] * 4,
        out_specs=(VMEM, VMEM),
        compiler_params=params(4),
        cost_estimate=cost(1),
        name="stack_pairs",
    )(a, b, c, d)


def forward(units, chips, x_own, x_other, pieces, carry=None):
    count, given = len(units), len(pieces)
    carry = list(carry) if carry else []

    def kernel(chip_of, xo, xt, *refs):
        parts, refs = refs[:given], refs[given + len(carry) :]
        acc_own, acc_other, panels, buf, tiles, ints, marks, sem_t, sem_b, sem_m = refs
        moved = []
        for t, pair in enumerate(units):
            for h, source in enumerate(pair):
                part, row, rows, at = source[-1]
                mark = row + MARK - at
                tile = pltpu.make_async_copy(parts[part].at[pl.ds(mark, 16)], tiles.at[2 * t + h], sem_t.at[2 * t + h])
                tile.start()
                moved.append(tile)
        for t, pair in enumerate(units):
            for h, source in enumerate(pair):
                for part, row, rows, at in source:
                    pltpu.make_async_copy(
                        parts[part].at[pl.ds(row, rows)], buf.at[t, h, pl.ds(at, rows)], sem_b.at[t, h]
                    ).start()
        if not carry:
            acc_own[...] = jnp.zeros_like(acc_own)
            acc_other[...] = jnp.zeros_like(acc_other)
        for i, m in enumerate(moved):
            m.wait()
            ints[pl.ds(i, 1), :] = tiles[i].astype(F32)[0:1].astype(jnp.int32)
        load = pltpu.make_async_copy(ints, marks, sem_m)
        load.start()
        load.wait()

        def step(t, _):
            for h in range(2):
                pltpu.make_async_copy(buf.at[t, h], buf.at[t, h], sem_b.at[t, h]).wait()
            panels[t] = jnp.zeros((NCB, 2 * BLK, BLK), BF16)
            for j in range(LIVE):
                h, k = divmod(j, HALF)
                pos = marks[2 * t + h, k]
                low = (pos >= NCB).astype(jnp.int32)
                panels[t, pos - low * NCB, pl.ds(pl.multiple_of(low * BLK, BLK), BLK), :] = buf[t, h, k * BLK : (k + 1) * BLK]
            cols = pl.ds(pl.multiple_of(chip_of[t] * 2 * BLK, 2 * BLK), 2 * BLK)
            x = jnp.concatenate([xo[:, cols], xt[:, cols]], axis=0)
            for c in range(NCB // 2):
                w = jnp.concatenate([panels[t, 2 * c], panels[t, 2 * c + 1]], axis=1)
                r = jnp.dot(x, w, preferred_element_type=F32)
                at = pl.ds(c * 2 * BLK, 2 * BLK)
                acc_own[:, at] += r[:BLK]
                acc_other[:, at] += r[BLK:]
            return 0

        lax.fori_loop(0, count, step, 0)

    acc = pltpu.VMEM((BLK, HID), F32)
    return pl.pallas_call(
        kernel,
        out_shape=(acc, acc, pltpu.VMEM((count, NCB, 2 * BLK, BLK), BF16)),
        in_specs=[SMEM, VMEM, VMEM] + [HBM] * given + [VMEM] * len(carry),
        out_specs=(VMEM, VMEM, VMEM),
        scratch_shapes=[
            pltpu.VMEM((count, 2, UNIT, BLK), BF16),
            pltpu.VMEM((2 * count, 16, BLK), BF16),
            pltpu.VMEM((2 * count, BLK), jnp.int32),
            pltpu.SMEM((2 * count, BLK), jnp.int32),
            pltpu.SemaphoreType.DMA((2 * count,)),
            pltpu.SemaphoreType.DMA((count, 2)),
            pltpu.SemaphoreType.DMA,
        ],
        input_output_aliases={3 + given + i: i for i in range(len(carry))},
        compiler_params=params(count + 3),
        cost_estimate=cost(1.6 * count + 2),
        name="forward",
    )(chips, x_own, x_other, *[pltpu.with_memory_space_constraint(p, pltpu.HBM) for p in pieces], *carry)


def act_kernel(scal, mine, got, d_hidden, hidden, d_mine, d_send):
    def work(gate_ref, up_ref, d_gate, d_up):
        for k in range(4):
            rel = pl.ds(k * ROWS, ROWS)
            real = pl.ds(pl.multiple_of((scal[1] - k + 4) % 4 * ROWS, ROWS), ROWS)
            gate, up = gate_ref[rel, :], up_ref[rel, :]
            d = d_hidden[real, :].astype(F32)
            sig = jax.nn.sigmoid(gate)
            active = gate * sig
            hidden[real, :] = (active * up).astype(BF16)
            d_gate[rel, :] = (d * up * sig * (1.0 + gate * (1.0 - sig))).astype(BF16)
            d_up[rel, :] = (d * active).astype(BF16)

    pl.when(scal[0] == 0)(lambda: work(mine, got, d_mine, d_send))
    pl.when(scal[0] != 0)(lambda: work(got, mine, d_send, d_mine))


def activate(scal, mine, got, d_hidden):
    one = pltpu.VMEM((BLK, HID), BF16)
    return pl.pallas_call(
        act_kernel,
        out_shape=(jax.ShapeDtypeStruct((BLK, HID), BF16), one, one),
        in_specs=[SMEM, VMEM, VMEM, VMEM],
        out_specs=(VMEM, VMEM, VMEM),
        compiler_params=params(8),
        cost_estimate=cost(4),
        name="activate",
    )(scal, mine, got, d_hidden)


def backward(d_own, d_other, panels):
    count = [p.shape[0] for p in panels]
    width = sum(count) * 2 * BLK

    def kernel(own, other, *refs):
        parts, (out_own, out_other, both) = refs[:-3], refs[-3:]
        both[:BLK] = own[...]
        both[BLK:] = other[...]
        done = 0
        for part, n in zip(parts, count):

            def step(t, _, part=part, done=done):
                w = jnp.concatenate([part[t, c] for c in range(NCB)], axis=1)
                r = lax.dot_general(both[...], w, (((1,), (1,)), ((), ())), preferred_element_type=F32)
                cols = pl.ds(pl.multiple_of((t + done) * 2 * BLK, 2 * BLK), 2 * BLK)
                out_own[:, cols] = r[:BLK]
                out_other[:, cols] = r[BLK:].astype(BF16)
                return 0

            lax.fori_loop(0, n, step, 0)
            done += n

    return pl.pallas_call(
        kernel,
        out_shape=(pltpu.VMEM((BLK, width), F32), pltpu.VMEM((BLK, width), BF16)),
        in_specs=[VMEM] * (2 + len(panels)),
        out_specs=(VMEM, VMEM),
        scratch_shapes=[pltpu.VMEM((2 * BLK, HID), BF16)],
        compiler_params=params(8),
        cost_estimate=cost(0.85 * sum(count) + 1),
        name="backward",
    )(d_own, d_other, *panels)


def join(owns, gots):
    cols = [p.shape[1] for p in owns]

    def kernel(*refs):
        n, outs = len(cols), refs[-4:]
        for k in range(4):
            at, start = slice(k * ROWS, (k + 1) * ROWS), 0
            for own, got, wide in zip(refs[:n], refs[n : 2 * n], cols):
                total = own[at, :] + got[at, :].astype(F32)
                outs[k][:, start : start + wide] = total.astype(outs[k].dtype)
                start += wide

    return pl.pallas_call(
        kernel,
        out_shape=(pltpu.VMEM((ROWS, sum(cols)), F32),) + (pltpu.VMEM((ROWS, sum(cols)), BF16),) * 3,
        in_specs=[VMEM] * (2 * len(cols)),
        out_specs=(VMEM,) * 4,
        compiler_params=params(4),
        cost_estimate=cost(1.5),
        name="join",
    )(*owns, *gots)


def finish(chips, groups):
    def kernel(chip_of, *refs):
        out, t = refs[-1], 0
        for g in range(len(groups)):
            parts = refs[4 * g : 4 * g + 4]
            for i in range(parts[0].shape[1] // (2 * BLK)):
                at = slice(i * 2 * BLK, (i + 1) * 2 * BLK)
                total = parts[0][:, at]
                for p in parts[1:]:
                    total += p[:, at].astype(F32)
                out[:, pl.ds(pl.multiple_of(chip_of[t] * 2 * BLK, 2 * BLK), 2 * BLK)] = total.astype(BF16)
                t += 1

    flat = [a for g in groups for a in g]
    return pl.pallas_call(
        kernel,
        out_shape=jax.ShapeDtypeStruct((ROWS, WIDTH), BF16),
        in_specs=[SMEM] + [VMEM] * len(flat),
        out_specs=VMEM,
        compiler_params=params(4),
        cost_estimate=cost(2),
        name="finish",
    )(chips, *flat)


def cost(us):
    return pl.CostEstimate(flops=int(us * 1.0e9), bytes_accessed=int(us * 3.0e6), transcendentals=0)


def shift(a, axis, by, name="near"):
    with jax.named_scope(name):
        return lax.ppermute(a, axis, [(i, (i + by) % 4) for i in range(4)])


def swap(a, name="swap"):
    with jax.named_scope(name):
        return lax.ppermute(a, "c", SWAP)


def together(*arrays):
    return lax.optimization_barrier(arrays)


def shards(tokens, gate_blocks, gate_index, up_blocks, up_index, d_hidden):
    x, y, core, z = (lax.axis_index(n) for n in ("x", "y", "c", "z"))
    first = core == 0
    gate_i, up_i = gate_index[0], up_index[0]
    theirs = swap(jnp.where(first, up_blocks[0], gate_blocks[0]), "swap_blocks")
    theirs_i = swap(jnp.where(first, up_i, gate_i), "swap_index")
    mine = jnp.where(first, gate_blocks[0], up_blocks[0])
    mine_i = jnp.where(first, gate_i, up_i)
    scal = jnp.stack([core, z, (x * 4 + y) * 2 * NCB])
    a, b = pack(scal[0::2], mine_i, theirs_i, mine, theirs)
    a, b, tokens = together(a, b, tokens)

    a1, b2, a2, b1 = shift(a, "x", 1, "a1"), shift(b, "y", -1, "b2"), shift(a, "x", -1, "a2"), shift(b, "y", 1, "b1")
    a1, b2 = together(a1, b2)
    a3, b3 = shift(a1, "x", 1, "a3"), shift(b2, "y", -1, "b3")
    pa, pb = stack_pairs(a, a1, b, b2)
    qa, qb = stack_pairs(a2, a3, b1, b3)
    t1 = shift(tokens, "z", 1, "tokens")
    near_tokens, t1 = together(tokens, t1)
    t3 = shift(near_tokens, "z", -1, "tokens")
    t1, t3 = together(t1, t3)
    t2 = shift(t1, "z", 1, "tokens")
    x_own = jnp.concatenate([tokens, t1, t2, t3], axis=0)
    x_other = swap(x_own, "swap_tokens")
    pa1, pb2 = together(shift(pa, "y", 1, "pa1"), shift(pb, "x", -1, "pb2"))
    qa2, qb1 = together(shift(qa, "y", -1, "qa2"), shift(qb, "x", 1, "qb1"))
    late_qa, late_qb, pa1, pb2 = together(qa, qb, pa1, pb2)
    qa1, qb2 = together(shift(late_qa, "y", 1, "qa1"), shift(late_qb, "x", -1, "qb2"))
    late_pa, late_pb, qa2, qb1 = together(pa, pb, qa2, qb1)
    pa2, pb1 = together(shift(late_pa, "y", -1, "pa2"), shift(late_pb, "x", 1, "pb1"))
    step = (0, -1, 1, 2)
    stages = (
        [(0, 0), (0, 1), (1, 1), (2, 0), (2, 2)],
        [(1, 0), (2, 1), (0, 2), (1, 2)],
        [(0, 3), (1, 3), (3, 0), (3, 2)],
        [(2, 3), (3, 1), (3, 3)],
    )
    order = [c for which in stages for c in which]
    chips = jnp.stack([(x + step[i]) % 4 * 4 + (y + step[j]) % 4 for i, j in order])
    held = {
        "a": [(a, a1, a2, a3), (pa1, None), (None, qa2), None, (0, 1, 2, 3)],
        "b": [(b, b1, b2, b3), (None, qb1), (pb2, None), None, (0, 2, 1, 3)],
    }

    def source(name, near, across):
        if across == 0:
            return [(held[name][0][near], 0, UNIT, 0)]
        half, row = divmod(held[name][4].index(near), 2)
        return [(held[name][across][half], row * UNIT, UNIT, 0)]

    def stage(which, at, carry=None):
        pieces, units = [], []
        for i, j in which:
            pair = []
            for src in (source("a", i, j), source("b", j, i)):
                row = []
                for piece, r, n, d in src:
                    k = next((m for m, p in enumerate(pieces) if p is piece), None)
                    if k is None:
                        k = len(pieces)
                        pieces.append(piece)
                    row.append((k, r, n, d))
                pair.append(row)
            units.append(pair)
        *carry, panels = forward(units, chips[at : at + len(which)], x_own, x_other, pieces, carry)
        return carry, panels

    carry, first_panels = stage(stages[0], 0)
    held_pa, held_pb, *carry = together(pa1, pb2, *carry)
    fpa, fpb = together(shift(held_pa, "y", 1, "fpa"), shift(held_pb, "x", -1, "fpb"))
    held_qa, held_qb, pa2, pb1 = together(qa2, qb1, pa2, pb1)
    fqa, fqb = together(shift(held_qa, "y", -1, "fqa"), shift(held_qb, "x", 1, "fqb"))
    held["a"][1:4] = (pa1, qa1), (pa2, qa2), (fpa, fqa)
    held["b"][1:4] = (pb1, qb1), (pb2, qb2), (fpb, fqb)
    panels, at = [first_panels], len(stages[0])
    for which in stages[1:]:
        carry, panel = stage(which, at, carry)
        panels.append(panel)
        at += len(which)
    acc_own, acc_other = carry
    got = swap(acc_other, "swap_gate_up")
    hidden, d_mine, d_send = activate(scal[:2], acc_own, got, d_hidden)
    d_other = swap(d_send, "swap_d")
    parts = []
    for some in (panels[2:], panels[:2]):
        part_own, part_other = backward(d_mine, d_other, some)
        parts.append((part_own, swap(part_other, "swap_part")))
    keep, *sends = join([p[0] for p in reversed(parts)], [p[1] for p in reversed(parts)])
    groups = [[keep] + [shift(s, "z", -k - 1, "send_back") for k, s in enumerate(sends)]]
    return hidden, finish(chips, groups)


def solution(mesh):
    fine = Mesh(mesh.devices.reshape(4, 4, 2, 4), ("x", "y", "c", "z"))
    fsdp = ("x", "y", "c")
    every = P((*fsdp, "z"), None)
    in_specs = (every, P("z", fsdp, None, None), P("z", fsdp), P("z", fsdp, None, None), P("z", fsdp), P(fsdp, "z"))
    return jax.shard_map(shards, mesh=fine, in_specs=in_specs, out_specs=(P(fsdp, "z"), every), check_vma=False)
```

```python
import jax
import jax.numpy as jnp
from jax import lax
from jax.experimental import pallas as pl
from jax.experimental.pallas import tpu as pltpu
from jax.sharding import Mesh, PartitionSpec as P

F32 = jnp.float32
BF16 = jnp.bfloat16
BLK = 128
CHIPS = 16
NCB = 28
CAP = 17
SURE = 11
LIVE = 28
HID = NCB * BLK
WIDTH = CHIPS * 2 * BLK
DEAD = 32 * NCB
SWAP = [(0, 1), (1, 0)]
HALF = LIVE // 2
UNIT = HALF * BLK + 16
MARK = HALF * BLK
ROWS = BLK // 4
HBM = pl.BlockSpec(memory_space=pltpu.HBM)
VMEM = pl.BlockSpec(memory_space=pltpu.VMEM)
SMEM = pl.BlockSpec(memory_space=pltpu.SMEM)


def params(mib=56):
    return pltpu.CompilerParams(vmem_limit_bytes=mib << 20)


def pack_kernel(scal, mine_i, theirs_i, mine, theirs, out_a, out_b):
    core, base = scal[0], scal[2]
    lane = lax.broadcasted_iota(jnp.int32, (16, BLK), 1)

    def place(j, block):
        out, at = (out_a, j) if j < HALF else (out_b, j - HALF)
        out[at * BLK : (at + 1) * BLK] = block

    def fill(first, first_i, second, second_i):
        n0 = jnp.int32(SURE)
        for j in range(SURE, CAP):
            n0 += (first_i[j] < DEAD).astype(jnp.int32)
        marks = [jnp.zeros((16, BLK), jnp.int32)] * 2
        for j in range(LIVE):
            if j < SURE:
                spot = first_i[j]
                place(j, first[j])
            elif j < CAP:
                spot = jnp.where(j < n0, first_i[j], second_i[jnp.maximum(j - n0, 0)])
                pl.when(j < n0)(lambda j=j: place(j, first[j]))
                pl.when(j >= n0)(lambda j=j: place(j, second[jnp.maximum(j - n0, 0)]))
            else:
                spot = second_i[j - n0]
                place(j, second[j - n0])
            half = j // HALF
            marks[half] = jnp.where(lane == j % HALF, spot - base, marks[half])
        out_a[MARK:UNIT] = marks[0].astype(F32).astype(BF16)
        out_b[MARK:UNIT] = marks[1].astype(F32).astype(BF16)

    pl.when(core == 0)(lambda: fill(mine, mine_i, theirs, theirs_i))
    pl.when(core != 0)(lambda: fill(theirs, theirs_i, mine, mine_i))


def pack(scal, mine_i, theirs_i, mine, theirs):
    one = jax.ShapeDtypeStruct((UNIT, BLK), BF16)
    return pl.pallas_call(
        pack_kernel,
        out_shape=(one, one),
        in_specs=[SMEM, SMEM, SMEM, VMEM, VMEM],
        out_specs=(VMEM, VMEM),
        compiler_params=params(8),
        cost_estimate=cost(2),
        name="pack",
    )(scal, mine_i, theirs_i, mine, theirs)


def stack_kernel(a, b, c, d, first, second):
    first[:UNIT] = a[...]
    first[UNIT:] = b[...]
    second[:UNIT] = c[...]
    second[UNIT:] = d[...]


def stack_pairs(a, b, c, d):
    two = pltpu.VMEM((2 * UNIT, BLK), BF16)
    return pl.pallas_call(
        stack_kernel,
        out_shape=(two, two),
        in_specs=[VMEM] * 4,
        out_specs=(VMEM, VMEM),
        compiler_params=params(4),
        cost_estimate=cost(1),
        name="stack_pairs",
    )(a, b, c, d)


def forward(units, at, chips, x_own, x_other, pieces, inside, carry=None):
    count, given = len(units), len(pieces)
    carry = list(carry) if carry else []

    def kernel(chip_of, xo, xt, *refs):
        parts, refs = refs[:given], refs[given + len(carry) :]
        acc_own, acc_other, panels, buf, tiles, ints, marks, sem_t, sem_b, sem_m = refs
        direct = all(inside)
        if not direct:
            moved = []
            for t, pair in enumerate(units):
                for h, source in enumerate(pair):
                    part, row, rows, to = source[-1]
                    mark = row + MARK - to
                    tile = pltpu.make_async_copy(parts[part].at[pl.ds(mark, 16)], tiles.at[2 * t + h], sem_t.at[2 * t + h])
                    tile.start()
                    moved.append(tile)
            for t, pair in enumerate(units):
                for h, source in enumerate(pair):
                    for part, row, rows, to in source:
                        pltpu.make_async_copy(
                            parts[part].at[pl.ds(row, rows)], buf.at[t, h, pl.ds(to, rows)], sem_b.at[t, h]
                        ).start()
        if not carry:
            acc_own[...] = jnp.zeros_like(acc_own)
            acc_other[...] = jnp.zeros_like(acc_other)
        for i in range(2 * count):
            if direct:
                part, row, rows, to = units[i // 2][i % 2][-1]
                tile = parts[part][row + MARK - to : row + UNIT - to]
            else:
                moved[i].wait()
                tile = tiles[i]
            ints[pl.ds(i, 1), :] = tile.astype(F32)[0:1].astype(jnp.int32)
        load = pltpu.make_async_copy(ints, marks, sem_m)
        load.start()
        load.wait()

        def block(t, h, k):
            if direct:
                part, row, rows, to = units[t][h][-1]
                return parts[part][row + k * BLK : row + (k + 1) * BLK]
            return buf[t, h, k * BLK : (k + 1) * BLK]

        def step(t, _):
            if not direct:
                for h in range(2):
                    pltpu.make_async_copy(buf.at[t, h], buf.at[t, h], sem_b.at[t, h]).wait()
            panels[t] = jnp.zeros((NCB, 2 * BLK, BLK), BF16)
            for j in range(LIVE):
                h, k = divmod(j, HALF)
                pos = marks[2 * t + h, k]
                low = (pos >= NCB).astype(jnp.int32)
                panels[t, pos - low * NCB, pl.ds(pl.multiple_of(low * BLK, BLK), BLK), :] = block(t, h, k)
            cols = pl.ds(pl.multiple_of(chip_of[at + t] * 2 * BLK, 2 * BLK), 2 * BLK)
            x = jnp.concatenate([xo[:, cols], xt[:, cols]], axis=0)
            for c in range(NCB // 2):
                w = jnp.concatenate([panels[t, 2 * c], panels[t, 2 * c + 1]], axis=1)
                r = jnp.dot(x, w, preferred_element_type=F32)
                span = pl.ds(c * 2 * BLK, 2 * BLK)
                acc_own[:, span] += r[:BLK]
                acc_other[:, span] += r[BLK:]
            return 0

        if direct:
            for t in range(count):
                step(t, 0)
        else:
            lax.fori_loop(0, count, step, 0)

    acc = pltpu.VMEM((BLK, HID), F32)
    return pl.pallas_call(
        kernel,
        out_shape=(acc, acc, pltpu.VMEM((count, NCB, 2 * BLK, BLK), BF16)),
        in_specs=[SMEM, VMEM, VMEM] + [VMEM if i else HBM for i in inside] + [VMEM] * len(carry),
        out_specs=(VMEM, VMEM, VMEM),
        scratch_shapes=[
            pltpu.VMEM((count, 2, UNIT, BLK), BF16),
            pltpu.VMEM((2 * count, 16, BLK), BF16),
            pltpu.VMEM((2 * count, BLK), jnp.int32),
            pltpu.SMEM((2 * count, BLK), jnp.int32),
            pltpu.SemaphoreType.DMA((2 * count,)),
            pltpu.SemaphoreType.DMA((count, 2)),
            pltpu.SemaphoreType.DMA,
        ],
        input_output_aliases={3 + given + i: i for i in range(len(carry))},
        compiler_params=params(count + 3),
        cost_estimate=cost(1.6 * count + 2),
        name="forward",
    )(chips, x_own, x_other, *[p if i else pltpu.with_memory_space_constraint(p, pltpu.HBM) for p, i in zip(pieces, inside)], *carry)


def act_kernel(scal, mine, got, d_hidden, hidden, d_mine, d_send):
    def work(gate_ref, up_ref, d_gate, d_up):
        for k in range(4):
            rel = pl.ds(k * ROWS, ROWS)
            real = pl.ds(pl.multiple_of((scal[1] - k + 4) % 4 * ROWS, ROWS), ROWS)
            gate, up = gate_ref[rel, :], up_ref[rel, :]
            d = d_hidden[real, :].astype(F32)
            sig = jax.nn.sigmoid(gate)
            active = gate * sig
            hidden[real, :] = (active * up).astype(BF16)
            d_gate[rel, :] = (d * up * sig * (1.0 + gate * (1.0 - sig))).astype(BF16)
            d_up[rel, :] = (d * active).astype(BF16)

    pl.when(scal[0] == 0)(lambda: work(mine, got, d_mine, d_send))
    pl.when(scal[0] != 0)(lambda: work(got, mine, d_send, d_mine))


def activate(scal, mine, got, d_hidden):
    one = pltpu.VMEM((BLK, HID), BF16)
    return pl.pallas_call(
        act_kernel,
        out_shape=(jax.ShapeDtypeStruct((BLK, HID), BF16), one, one),
        in_specs=[SMEM, VMEM, VMEM, VMEM],
        out_specs=(VMEM, VMEM, VMEM),
        compiler_params=params(8),
        cost_estimate=cost(4),
        name="activate",
    )(scal, mine, got, d_hidden)


def backward(d_own, d_other, panels):
    count = [p.shape[0] for p in panels]
    width = sum(count) * 2 * BLK

    def kernel(own, other, *refs):
        parts, (out_own, out_other, both) = refs[:-3], refs[-3:]
        both[:BLK] = own[...]
        both[BLK:] = other[...]
        done = 0
        for part, n in zip(parts, count):

            def step(t, _, part=part, done=done):
                w = jnp.concatenate([part[t, c] for c in range(NCB)], axis=1)
                r = lax.dot_general(both[...], w, (((1,), (1,)), ((), ())), preferred_element_type=F32)
                cols = pl.ds(pl.multiple_of((t + done) * 2 * BLK, 2 * BLK), 2 * BLK)
                out_own[:, cols] = r[:BLK]
                out_other[:, cols] = r[BLK:].astype(BF16)
                return 0

            lax.fori_loop(0, n, step, 0)
            done += n

    return pl.pallas_call(
        kernel,
        out_shape=(pltpu.VMEM((BLK, width), F32), pltpu.VMEM((BLK, width), BF16)),
        in_specs=[VMEM] * (2 + len(panels)),
        out_specs=(VMEM, VMEM),
        scratch_shapes=[pltpu.VMEM((2 * BLK, HID), BF16)],
        compiler_params=params(8),
        cost_estimate=cost(0.85 * sum(count) + 1),
        name="backward",
    )(d_own, d_other, *panels)


def join(owns, gots):
    cols = [p.shape[1] for p in owns]

    def kernel(*refs):
        n, outs = len(cols), refs[-4:]
        for k in range(4):
            at, start = slice(k * ROWS, (k + 1) * ROWS), 0
            for own, got, wide in zip(refs[:n], refs[n : 2 * n], cols):
                total = own[at, :] + got[at, :].astype(F32)
                outs[k][:, start : start + wide] = total.astype(outs[k].dtype)
                start += wide

    return pl.pallas_call(
        kernel,
        out_shape=(pltpu.VMEM((ROWS, sum(cols)), F32),) + (pltpu.VMEM((ROWS, sum(cols)), BF16),) * 3,
        in_specs=[VMEM] * (2 * len(cols)),
        out_specs=(VMEM,) * 4,
        compiler_params=params(4),
        cost_estimate=cost(1.5),
        name="join",
    )(*owns, *gots)


def finish(chips, groups):
    def kernel(chip_of, *refs):
        out, t = refs[-1], 0
        for g in range(len(groups)):
            parts = refs[4 * g : 4 * g + 4]
            for i in range(parts[0].shape[1] // (2 * BLK)):
                at = slice(i * 2 * BLK, (i + 1) * 2 * BLK)
                total = parts[0][:, at]
                for p in parts[1:]:
                    total += p[:, at].astype(F32)
                out[:, pl.ds(pl.multiple_of(chip_of[t] * 2 * BLK, 2 * BLK), 2 * BLK)] = total.astype(BF16)
                t += 1

    flat = [a for g in groups for a in g]
    return pl.pallas_call(
        kernel,
        out_shape=jax.ShapeDtypeStruct((ROWS, WIDTH), BF16),
        in_specs=[SMEM] + [VMEM] * len(flat),
        out_specs=VMEM,
        compiler_params=params(4),
        cost_estimate=cost(2),
        name="finish",
    )(chips, *flat)


def cost(us):
    return pl.CostEstimate(flops=int(us * 1.0e9), bytes_accessed=int(us * 3.0e6), transcendentals=0)


def shift(a, axis, by, name="near"):
    with jax.named_scope(name):
        return lax.ppermute(a, axis, [(i, (i + by) % 4) for i in range(4)])


def swap(a, name="swap"):
    with jax.named_scope(name):
        return lax.ppermute(a, "c", SWAP)


def together(*arrays):
    return lax.optimization_barrier(arrays)


def shards(tokens, gate_blocks, gate_index, up_blocks, up_index, d_hidden):
    x, y, core, z = (lax.axis_index(n) for n in ("x", "y", "c", "z"))
    first = core == 0
    gate_i, up_i = gate_index[0], up_index[0]
    theirs = swap(jnp.where(first, up_blocks[0], gate_blocks[0]), "swap_blocks")
    theirs_i = swap(jnp.where(first, up_i, gate_i), "swap_index")
    mine = jnp.where(first, gate_blocks[0], up_blocks[0])
    mine_i = jnp.where(first, gate_i, up_i)
    step = (0, -1, 1, 2)
    stages = (
        [(0, 0), (0, 1), (1, 1), (2, 0), (2, 2)],
        [(1, 0), (3, 0), (0, 2), (1, 2), (3, 2), (0, 3), (1, 3)],
        [(2, 1), (3, 1), (2, 3), (3, 3)],
    )
    order = [c for which in stages for c in which]
    chips = jnp.stack([(x + step[i]) % 4 * 4 + (y + step[j]) % 4 for i, j in order])
    scal = jnp.stack([core, z, (x * 4 + y) * 2 * NCB])
    a, b = pack(scal, mine_i, theirs_i, mine, theirs)
    a, b, chips, scal, near_tokens = together(a, b, chips, scal, tokens)

    a1, b2, a2, b1 = shift(a, "x", 1, "a1"), shift(b, "y", -1, "b2"), shift(a, "x", -1, "a2"), shift(b, "y", 1, "b1")
    t1 = shift(near_tokens, "z", 1, "tokens")
    a1, b2 = together(a1, b2)
    tokens, t1, a2, b1 = together(tokens, t1, a2, b1)
    a3, b3 = shift(a1, "x", 1, "a3"), shift(b2, "y", -1, "b3")
    t2, t3 = shift(t1, "z", 1, "tokens"), shift(tokens, "z", -1, "tokens")
    t2, t3, a3, b3 = together(t2, t3, a3, b3)
    qa, qb = stack_pairs(a2, a3, b1, b3)
    qa, qb, a_late, b_late = together(qa, qb, a, b)
    pa, pb = stack_pairs(a_late, a1, b_late, b2)
    qa2, qb1 = shift(qa, "y", -1, "qa2"), shift(qb, "x", 1, "qb1")
    pa1, pb2 = shift(pa, "y", 1, "pa1"), shift(pb, "x", -1, "pb2")
    x_own = jnp.concatenate([tokens, t1, t2, t3], axis=0)
    x_other = swap(x_own, "swap_tokens")
    late_pa, qa2, pa1 = together(pa, qa2, pa1)
    late_pb, qb1, pb2 = together(pb, qb1, pb2)
    pa2, pb1 = shift(late_pa, "y", -1, "pa2"), shift(late_pb, "x", 1, "pb1")
    fpa, fpb = shift(pa1, "y", 1, "fpa"), shift(pb2, "x", -1, "fpb")
    held = {
        "a": [(a, a1, a2, a3), (pa1, None), (pa2, qa2), (fpa, None), (0, 1, 2, 3)],
        "b": [(b, b1, b2, b3), (pb1, qb1), (pb2, None), (fpb, None), (0, 2, 1, 3)],
    }

    def source(name, near, across):
        if across == 0:
            return [(held[name][0][near], 0, UNIT, 0)]
        half, row = divmod(held[name][4].index(near), 2)
        return [(held[name][across][half], row * UNIT, UNIT, 0)]

    def stage(which, at, carry=None, fresh=()):
        pieces, units = [], []
        for i, j in which:
            pair = []
            for src in (source("a", i, j), source("b", j, i)):
                row = []
                for piece, r, n, d in src:
                    k = next((m for m, p in enumerate(pieces) if p is piece), None)
                    if k is None:
                        k = len(pieces)
                        pieces.append(piece)
                    row.append((k, r, n, d))
                pair.append(row)
            units.append(pair)
        *carry, panels = forward(units, at, chips, x_own, x_other, pieces, [any(p is f for f in fresh) for p in pieces], carry)
        return carry, panels

    carry, first_panels = stage(stages[0], 0)
    late_qa, late_qb, held_qa, held_qb, *carry = together(qa, qb, qa2, qb1, *carry)
    late_qa, held_qa, fpa, pa2 = together(late_qa, held_qa, fpa, pa2)
    late_qb, held_qb, fpb, pb1 = together(late_qb, held_qb, fpb, pb1)
    fqa, fqb = shift(held_qa, "y", -1, "fqa"), shift(held_qb, "x", 1, "fqb")
    qa1, qb2 = shift(late_qa, "y", 1, "qa1"), shift(late_qb, "x", -1, "qb2")
    held["a"][1:4] = (pa1, qa1), (pa2, qa2), (fpa, fqa)
    held["b"][1:4] = (pb1, qb1), (pb2, qb2), (fpb, fqb)
    panels, at = [first_panels], len(stages[0])
    for which in stages[1:]:
        carry, panel = stage(which, at, carry, (qa1, qb2, fqa, fqb))
        panels.append(panel)
        at += len(which)
    acc_own, acc_other = carry
    got = swap(acc_other, "swap_gate_up")
    hidden, d_mine, d_send = activate(scal, acc_own, got, d_hidden)
    d_other = swap(d_send, "swap_d")
    parts = []
    for some in (panels[1:2], panels[0::2]):
        part_own, part_other = backward(d_mine, d_other, some)
        parts.append((part_own, swap(part_other, "swap_part")))
    keep, *sends = join([p[0] for p in parts], [p[1] for p in parts])
    tail = [c for k in (1, 0, 2) for c in stages[k]]
    tail = jnp.stack([(x + step[i]) % 4 * 4 + (y + step[j]) % 4 for i, j in tail])
    groups = [[keep] + [shift(s, "z", -k - 1, "send_back") for k, s in enumerate(sends)]]
    return hidden, finish(tail, groups)


def solution(mesh):
    fine = Mesh(mesh.devices.reshape(4, 4, 2, 4), ("x", "y", "c", "z"))
    fsdp = ("x", "y", "c")
    every = P((*fsdp, "z"), None)
    in_specs = (every, P("z", fsdp, None, None), P("z", fsdp), P("z", fsdp, None, None), P("z", fsdp), P(fsdp, "z"))
    return jax.shard_map(shards, mesh=fine, in_specs=in_specs, out_specs=(P(fsdp, "z"), every), check_vma=False)
```

```python
import jax
import jax.numpy as jnp
from jax import lax
from jax.experimental import pallas as pl
from jax.experimental.pallas import tpu as pltpu
from jax.sharding import Mesh, PartitionSpec as P

F32 = jnp.float32
BF16 = jnp.bfloat16
BLK = 128
CHIPS = 16
NCB = 28
CAP = 17
SURE = 11
LIVE = 28
HID = NCB * BLK
WIDTH = CHIPS * 2 * BLK
DEAD = 32 * NCB
SWAP = [(0, 1), (1, 0)]
HALF = LIVE // 2
UNIT = HALF * BLK + 16
MARK = HALF * BLK
ROWS = BLK // 4
HBM = pl.BlockSpec(memory_space=pltpu.HBM)
VMEM = pl.BlockSpec(memory_space=pltpu.VMEM)
SMEM = pl.BlockSpec(memory_space=pltpu.SMEM)


def params(mib=56):
    return pltpu.CompilerParams(vmem_limit_bytes=mib << 20)


def pack_kernel(scal, mine_i, theirs_i, mine, theirs, out_a, out_b):
    core, base = scal[0], scal[2]
    lane = lax.broadcasted_iota(jnp.int32, (16, BLK), 1)

    def place(j, block):
        out, at = (out_a, j) if j < HALF else (out_b, j - HALF)
        out[at * BLK : (at + 1) * BLK] = block

    def fill(first, first_i, second, second_i):
        n0 = jnp.int32(SURE)
        for j in range(SURE, CAP):
            n0 += (first_i[j] < DEAD).astype(jnp.int32)
        marks = [jnp.zeros((16, BLK), jnp.int32)] * 2
        for j in range(LIVE):
            if j < SURE:
                spot = first_i[j]
                place(j, first[j])
            elif j < CAP:
                spot = jnp.where(j < n0, first_i[j], second_i[jnp.maximum(j - n0, 0)])
                pl.when(j < n0)(lambda j=j: place(j, first[j]))
                pl.when(j >= n0)(lambda j=j: place(j, second[jnp.maximum(j - n0, 0)]))
            else:
                spot = second_i[j - n0]
                place(j, second[j - n0])
            half = j // HALF
            marks[half] = jnp.where(lane == j % HALF, spot - base, marks[half])
        out_a[MARK:UNIT] = marks[0].astype(F32).astype(BF16)
        out_b[MARK:UNIT] = marks[1].astype(F32).astype(BF16)

    pl.when(core == 0)(lambda: fill(mine, mine_i, theirs, theirs_i))
    pl.when(core != 0)(lambda: fill(theirs, theirs_i, mine, mine_i))


def pack(scal, mine_i, theirs_i, mine, theirs):
    one = jax.ShapeDtypeStruct((UNIT, BLK), BF16)
    return pl.pallas_call(
        pack_kernel,
        out_shape=(one, one),
        in_specs=[SMEM, SMEM, SMEM, VMEM, VMEM],
        out_specs=(VMEM, VMEM),
        compiler_params=params(8),
        cost_estimate=cost(2),
        name="pack",
    )(scal, mine_i, theirs_i, mine, theirs)


def stack_kernel(a, b, c, d, first, second):
    first[:UNIT] = a[...]
    first[UNIT:] = b[...]
    second[:UNIT] = c[...]
    second[UNIT:] = d[...]


def stack_pairs(a, b, c, d):
    two = pltpu.VMEM((2 * UNIT, BLK), BF16)
    return pl.pallas_call(
        stack_kernel,
        out_shape=(two, two),
        in_specs=[VMEM] * 4,
        out_specs=(VMEM, VMEM),
        compiler_params=params(4),
        cost_estimate=cost(1),
        name="stack_pairs",
    )(a, b, c, d)


def forward(units, at, chips, x_own, x_other, pieces, inside, carry=None):
    count, given = len(units), len(pieces)
    carry = list(carry) if carry else []

    def kernel(chip_of, xo, xt, *refs):
        parts, refs = refs[:given], refs[given + len(carry) :]
        acc_own, *acc_other, panels, buf, tiles, ints, marks, sem_t, sem_b, sem_m = refs
        direct = all(inside)
        if not direct:
            moved = []
            for t, pair in enumerate(units):
                for h, source in enumerate(pair):
                    part, row, rows, to = source[-1]
                    mark = row + MARK - to
                    tile = pltpu.make_async_copy(parts[part].at[pl.ds(mark, 16)], tiles.at[2 * t + h], sem_t.at[2 * t + h])
                    tile.start()
                    moved.append(tile)
            for t, pair in enumerate(units):
                for h, source in enumerate(pair):
                    for part, row, rows, to in source:
                        pltpu.make_async_copy(
                            parts[part].at[pl.ds(row, rows)], buf.at[t, h, pl.ds(to, rows)], sem_b.at[t, h]
                        ).start()
        if not carry:
            acc_own[...] = jnp.zeros_like(acc_own)
            for acc in acc_other:
                acc[...] = jnp.zeros_like(acc)
        for i in range(2 * count):
            if direct:
                part, row, rows, to = units[i // 2][i % 2][-1]
                tile = parts[part][row + MARK - to : row + UNIT - to]
            else:
                moved[i].wait()
                tile = tiles[i]
            ints[pl.ds(i, 1), :] = tile.astype(F32)[0:1].astype(jnp.int32)
        load = pltpu.make_async_copy(ints, marks, sem_m)
        load.start()
        load.wait()

        def block(t, h, k):
            if direct:
                part, row, rows, to = units[t][h][-1]
                return parts[part][row + k * BLK : row + (k + 1) * BLK]
            return buf[t, h, k * BLK : (k + 1) * BLK]

        def step(t, _):
            if not direct:
                for h in range(2):
                    pltpu.make_async_copy(buf.at[t, h], buf.at[t, h], sem_b.at[t, h]).wait()
            panels[t] = jnp.zeros((NCB, 2 * BLK, BLK), BF16)
            for j in range(LIVE):
                h, k = divmod(j, HALF)
                pos = marks[2 * t + h, k]
                low = (pos >= NCB).astype(jnp.int32)
                panels[t, pos - low * NCB, pl.ds(pl.multiple_of(low * BLK, BLK), BLK), :] = block(t, h, k)
            cols = pl.ds(pl.multiple_of(chip_of[at + t] * 2 * BLK, 2 * BLK), 2 * BLK)
            x = jnp.concatenate([xo[:, cols], xt[:, cols]], axis=0)
            for c in range(NCB // 2):
                w = jnp.concatenate([panels[t, 2 * c], panels[t, 2 * c + 1]], axis=1)
                r = jnp.dot(x, w, preferred_element_type=F32)
                span = pl.ds(c * 2 * BLK, 2 * BLK)
                acc_own[:, span] += r[:BLK]
                there = pl.ds(c % (NCB // 4) * 2 * BLK, 2 * BLK)
                acc_other[c // (NCB // 4)][:, there] += r[BLK:]
            return 0

        if direct:
            for t in range(count):
                step(t, 0)
        else:
            lax.fori_loop(0, count, step, 0)

    acc, half = pltpu.VMEM((BLK, HID), F32), pltpu.VMEM((BLK, HID // 2), F32)
    return pl.pallas_call(
        kernel,
        out_shape=(acc, half, half, pltpu.VMEM((count, NCB, 2 * BLK, BLK), BF16)),
        in_specs=[SMEM, VMEM, VMEM] + [VMEM if i else HBM for i in inside] + [VMEM] * len(carry),
        out_specs=(VMEM,) * 4,
        scratch_shapes=[
            pltpu.VMEM((count, 2, UNIT, BLK), BF16),
            pltpu.VMEM((2 * count, 16, BLK), BF16),
            pltpu.VMEM((2 * count, BLK), jnp.int32),
            pltpu.SMEM((2 * count, BLK), jnp.int32),
            pltpu.SemaphoreType.DMA((2 * count,)),
            pltpu.SemaphoreType.DMA((count, 2)),
            pltpu.SemaphoreType.DMA,
        ],
        input_output_aliases={3 + given + i: i for i in range(len(carry))},
        compiler_params=params(count + 3),
        cost_estimate=cost(1.6 * count + 2),
        name="forward",
    )(chips, x_own, x_other, *[p if i else pltpu.with_memory_space_constraint(p, pltpu.HBM) for p, i in zip(pieces, inside)], *carry)


def activate(half, scal, mine, got, d_hidden):
    wide = HID // 2
    part = slice(half * wide, (half + 1) * wide)

    def kernel(scal, mine, got, d_hidden, hidden, d_mine, d_send):
        def work(gate_of, up_of, d_gate, d_up):
            for k in range(4):
                rel = pl.ds(k * ROWS, ROWS)
                real = pl.ds(pl.multiple_of((scal[1] - k + 4) % 4 * ROWS, ROWS), ROWS)
                gate, up = gate_of(rel), up_of(rel)
                d = d_hidden[real, part].astype(F32)
                sig = jax.nn.sigmoid(gate)
                active = gate * sig
                hidden[real, :] = (active * up).astype(BF16)
                d_gate[rel, :] = (d * up * sig * (1.0 + gate * (1.0 - sig))).astype(BF16)
                d_up[rel, :] = (d * active).astype(BF16)

        here, there = (lambda rows: mine[rows, part]), (lambda rows: got[rows, :])
        pl.when(scal[0] == 0)(lambda: work(here, there, d_mine, d_send))
        pl.when(scal[0] != 0)(lambda: work(there, here, d_send, d_mine))

    one = pltpu.VMEM((BLK, wide), BF16)
    return pl.pallas_call(
        kernel,
        out_shape=(one, one, one),
        in_specs=[SMEM, VMEM, VMEM, VMEM],
        out_specs=(VMEM, VMEM, VMEM),
        compiler_params=params(8),
        cost_estimate=cost(2),
        name="activate",
    )(scal, mine, got, d_hidden)


def backward(d_own, d_other, panels):
    count = [p.shape[0] for p in panels]
    width = sum(count) * 2 * BLK

    def kernel(*refs):
        parts, (out_own, out_other, both) = refs[4:-3], refs[-3:]
        for i in range(4):
            both[i // 2 * BLK : (i // 2 + 1) * BLK, i % 2 * (HID // 2) : (i % 2 + 1) * (HID // 2)] = refs[i][...]
        done = 0
        for part, n in zip(parts, count):

            def step(t, _, part=part, done=done):
                w = jnp.concatenate([part[t, c] for c in range(NCB)], axis=1)
                r = lax.dot_general(both[...], w, (((1,), (1,)), ((), ())), preferred_element_type=F32)
                cols = pl.ds(pl.multiple_of((t + done) * 2 * BLK, 2 * BLK), 2 * BLK)
                out_own[:, cols] = r[:BLK]
                out_other[:, cols] = r[BLK:].astype(BF16)
                return 0

            lax.fori_loop(0, n, step, 0, unroll=True)
            done += n

    return pl.pallas_call(
        kernel,
        out_shape=(pltpu.VMEM((BLK, width), F32), pltpu.VMEM((BLK, width), BF16)),
        in_specs=[VMEM] * (4 + len(panels)),
        out_specs=(VMEM, VMEM),
        scratch_shapes=[pltpu.VMEM((2 * BLK, HID), BF16)],
        compiler_params=params(8),
        cost_estimate=cost(0.85 * sum(count) + 1),
        name="backward",
    )(*d_own, *d_other, *panels)


def join(owns, gots):
    cols = [p.shape[1] for p in owns]

    def kernel(*refs):
        n, outs = len(cols), refs[-4:]
        for k in range(4):
            at, start = slice(k * ROWS, (k + 1) * ROWS), 0
            for own, got, wide in zip(refs[:n], refs[n : 2 * n], cols):
                total = own[at, :] + got[at, :].astype(F32)
                outs[k][:, start : start + wide] = total.astype(outs[k].dtype)
                start += wide

    return pl.pallas_call(
        kernel,
        out_shape=(pltpu.VMEM((ROWS, sum(cols)), F32),) + (pltpu.VMEM((ROWS, sum(cols)), BF16),) * 3,
        in_specs=[VMEM] * (2 * len(cols)),
        out_specs=(VMEM,) * 4,
        compiler_params=params(4),
        cost_estimate=cost(1.5),
        name="join",
    )(*owns, *gots)


def finish(chips, groups):
    def kernel(chip_of, *refs):
        out, t = refs[-1], 0
        for g in range(len(groups)):
            parts = refs[4 * g : 4 * g + 4]
            for i in range(parts[0].shape[1] // (2 * BLK)):
                at = slice(i * 2 * BLK, (i + 1) * 2 * BLK)
                total = parts[0][:, at]
                for p in parts[1:]:
                    total += p[:, at].astype(F32)
                out[:, pl.ds(pl.multiple_of(chip_of[t] * 2 * BLK, 2 * BLK), 2 * BLK)] = total.astype(BF16)
                t += 1

    flat = [a for g in groups for a in g]
    return pl.pallas_call(
        kernel,
        out_shape=jax.ShapeDtypeStruct((ROWS, WIDTH), BF16),
        in_specs=[SMEM] + [VMEM] * len(flat),
        out_specs=VMEM,
        compiler_params=params(4),
        cost_estimate=cost(2),
        name="finish",
    )(chips, *flat)


def cost(us):
    return pl.CostEstimate(flops=int(us * 1.0e9), bytes_accessed=int(us * 3.0e6), transcendentals=0)


def shift(a, axis, by, name="near"):
    with jax.named_scope(name):
        return lax.ppermute(a, axis, [(i, (i + by) % 4) for i in range(4)])


def swap(a, name="swap"):
    with jax.named_scope(name):
        return lax.ppermute(a, "c", SWAP)


def together(*arrays):
    return lax.optimization_barrier(arrays)


def shards(tokens, gate_blocks, gate_index, up_blocks, up_index, d_hidden):
    x, y, core, z = (lax.axis_index(n) for n in ("x", "y", "c", "z"))
    first = core == 0
    gate_i, up_i = gate_index[0], up_index[0]
    theirs = swap(jnp.where(first, up_blocks[0], gate_blocks[0]), "swap_blocks")
    theirs_i = swap(jnp.where(first, up_i, gate_i), "swap_index")
    mine = jnp.where(first, gate_blocks[0], up_blocks[0])
    mine_i = jnp.where(first, gate_i, up_i)
    step = (0, -1, 1, 2)
    stages = (
        [(0, 0), (0, 1), (1, 1), (2, 0), (2, 2)],
        [(1, 0), (3, 0), (0, 2), (1, 2), (3, 2), (0, 3), (1, 3)],
        [(2, 1), (3, 1), (2, 3), (3, 3)],
    )
    order = [c for which in stages for c in which]
    chips = jnp.stack([(x + step[i]) % 4 * 4 + (y + step[j]) % 4 for i, j in order])
    scal = jnp.stack([core, z, (x * 4 + y) * 2 * NCB])
    a, b = pack(scal, mine_i, theirs_i, mine, theirs)
    a, b, chips, scal, near_tokens = together(a, b, chips, scal, tokens)

    a1, b2, a2, b1 = shift(a, "x", 1, "a1"), shift(b, "y", -1, "b2"), shift(a, "x", -1, "a2"), shift(b, "y", 1, "b1")
    t1 = shift(near_tokens, "z", 1, "tokens")
    a1, b2 = together(a1, b2)
    tokens, t1, a2, b1 = together(tokens, t1, a2, b1)
    a3, b3 = shift(a1, "x", 1, "a3"), shift(b2, "y", -1, "b3")
    t2, t3 = shift(t1, "z", 1, "tokens"), shift(tokens, "z", -1, "tokens")
    t2, t3, a3, b3 = together(t2, t3, a3, b3)
    qa, qb = stack_pairs(a2, a3, b1, b3)
    qa, qb, a_late, b_late = together(qa, qb, a, b)
    pa, pb = stack_pairs(a_late, a1, b_late, b2)
    qa2, qb1 = shift(qa, "y", -1, "qa2"), shift(qb, "x", 1, "qb1")
    pa1, pb2 = shift(pa, "y", 1, "pa1"), shift(pb, "x", -1, "pb2")
    x_own = jnp.concatenate([tokens, t1, t2, t3], axis=0)
    x_other = swap(x_own, "swap_tokens")
    late_pa, qa2, pa1 = together(pa, qa2, pa1)
    late_pb, qb1, pb2 = together(pb, qb1, pb2)
    pa2, pb1 = shift(late_pa, "y", -1, "pa2"), shift(late_pb, "x", 1, "pb1")
    fpa, fpb = shift(pa1, "y", 1, "fpa"), shift(pb2, "x", -1, "fpb")
    held = {
        "a": [(a, a1, a2, a3), (pa1, None), (pa2, qa2), (fpa, None), (0, 1, 2, 3)],
        "b": [(b, b1, b2, b3), (pb1, qb1), (pb2, None), (fpb, None), (0, 2, 1, 3)],
    }

    def source(name, near, across):
        if across == 0:
            return [(held[name][0][near], 0, UNIT, 0)]
        half, row = divmod(held[name][4].index(near), 2)
        return [(held[name][across][half], row * UNIT, UNIT, 0)]

    def stage(which, at, carry=None, fresh=()):
        pieces, units = [], []
        for i, j in which:
            pair = []
            for src in (source("a", i, j), source("b", j, i)):
                row = []
                for piece, r, n, d in src:
                    k = next((m for m, p in enumerate(pieces) if p is piece), None)
                    if k is None:
                        k = len(pieces)
                        pieces.append(piece)
                    row.append((k, r, n, d))
                pair.append(row)
            units.append(pair)
        *carry, panels = forward(units, at, chips, x_own, x_other, pieces, [any(p is f for f in fresh) for p in pieces], carry)
        return carry, panels

    carry, first_panels = stage(stages[0], 0)
    late_qa, late_qb, held_qa, held_qb, *carry = together(qa, qb, qa2, qb1, *carry)
    late_qa, held_qa, fpa, pa2 = together(late_qa, held_qa, fpa, pa2)
    late_qb, held_qb, fpb, pb1 = together(late_qb, held_qb, fpb, pb1)
    fqa, fqb = shift(held_qa, "y", -1, "fqa"), shift(held_qb, "x", 1, "fqb")
    qa1, qb2 = shift(late_qa, "y", 1, "qa1"), shift(late_qb, "x", -1, "qb2")
    held["a"][1:4] = (pa1, qa1), (pa2, qa2), (fpa, fqa)
    held["b"][1:4] = (pb1, qb1), (pb2, qb2), (fpb, fqb)
    panels, at = [first_panels], len(stages[0])
    for which in stages[1:]:
        carry, panel = stage(which, at, carry, (qa1, qb2, fqa, fqb))
        panels.append(panel)
        at += len(which)
    acc_own, *acc_other = carry
    got = [swap(acc, "swap_gate_up") for acc in acc_other]
    done = [activate(half, scal, acc_own, got[half], d_hidden) for half in range(2)]
    hidden = jnp.concatenate([d[0] for d in done], axis=1)
    d_mine, d_other = [d[1] for d in done], [swap(d[2], "swap_d") for d in done]
    parts = []
    for some in (panels[1::-1], panels[2:]):
        part_own, part_other = backward(d_mine, d_other, some)
        parts.append((part_own, swap(part_other, "swap_part")))
    keep, *sends = join([p[0] for p in parts], [p[1] for p in parts])
    tail = [c for k in (1, 0, 2) for c in stages[k]]
    tail = jnp.stack([(x + step[i]) % 4 * 4 + (y + step[j]) % 4 for i, j in tail])
    groups = [[keep] + [shift(s, "z", -k - 1, "send_back") for k, s in enumerate(sends)]]
    return hidden, finish(tail, groups)


def solution(mesh):
    fine = Mesh(mesh.devices.reshape(4, 4, 2, 4), ("x", "y", "c", "z"))
    fsdp = ("x", "y", "c")
    every = P((*fsdp, "z"), None)
    in_specs = (every, P("z", fsdp, None, None), P("z", fsdp), P("z", fsdp, None, None), P("z", fsdp), P(fsdp, "z"))
    return jax.shard_map(shards, mesh=fine, in_specs=in_specs, out_specs=(P(fsdp, "z"), every), check_vma=False)
```
